128 devices in a mesh: dp: 2 (over core), blk: 32 (over z_hi, x, y), head: 2 (over z_lo).
Axes of the slice: x: 4, y: 4, z: 4 (z_hi: 2, z_lo: 2; z = z_hi * 2 + z_lo), core: 2. Of those that a mesh axis runs over, the one named last changes fastest.
Arguments:
- stored_query_rows: bfloat16 [16384, 8192], P(('dp', 'blk', 'head')), parts along dimension 0
- stored_key_rows: bfloat16 [16384, 1024], P(('dp', 'blk', 'head')), parts along dimension 0
- stored_value_rows: bfloat16 [16384, 1024], P(('dp', 'blk', 'head')), parts along dimension 0, may hold values from -6 to 6
- block_docs: int32 [128], P('dp'), parts along dimension 0, may hold values from 0 to 15, never falling along the last dimension, each value on 1 to 8 neighbouring positions
Outputs:
- context: bfloat16 [16384, 8192], P(('dp', 'blk', 'head')), parts along dimension 0
The draws below stay inside these ranges and needn't reach their ends.
There are 2 independent parts, one for each index of `dp`. The reference program is written for one: setup_inputs(seed, part) draws one part's arguments, and reference() takes and returns one part's arrays. A program takes and returns all parts, laid end to end along the dimension named above; each array names one. Nothing has to cross between parts.
Inputs may be any that keep to these rules, and one draw needn't show every extreme that they name: `block_docs`: document numbers never fall along the sequence; each document covers 1 to 8 blocks, and one covers exactly 8.
All inputs are finite; a program needn't handle non-finite values.
Results may differ from the reference program's by a relative error of at most 0.0045.
Values may be sent and summed in bfloat16 or wider, within the bound.
A program may use at most 128 MiB of HBM per device.

```python
import math
import jax
import jax.numpy as jnp
import numpy as np
from jax import lax

QUERY_HEADS = 64
KEY_VALUE_HEADS = 8
HEAD_DIMENSION = 128
MASK_BLOCK_SIZE = 128
TOK_DEV = 128
PACKED_TOKENS = 8192
NBLOCKS = 64
DOC_BLOCKS = 8
DOCS = 16
N_BLK = 32


def shared_keys(key):
    block_section = jax.random.fold_in(key, 11)
    block_offset = jax.random.normal(block_section, (PACKED_TOKENS, KEY_VALUE_HEADS * HEAD_DIMENSION), jnp.float32)
    return block_offset


def draw_stored_key_rows(key, part):
    block_offset = shared_keys(key)
    return block_offset.astype(jnp.bfloat16)


def draw_stored_query_rows(key, part):
    block_section = jax.random.fold_in(key, 13)
    drawn = jax.random.normal(block_section, (PACKED_TOKENS, QUERY_HEADS * HEAD_DIMENSION), jnp.float32)
    return drawn.astype(jnp.bfloat16)


def levels(rng, dims, split, least, largest):
    gain, own = 1.0, jax.random.fold_in(rng, 6)
    for dim, parts in split:
        steps = jnp.exp(jax.random.uniform(jax.random.fold_in(own, dim), (parts,), jnp.float32, least / len(split), largest / len(split)))
        gain = gain * jnp.repeat(steps, dims[dim] // parts).reshape([-1 if axis == dim else 1 for axis in range(len(dims))])
    return gain


def split_up(count, total, most, slope):
    weights = [(1 << 20) // math.isqrt(grade ** slope) + 1 for grade in range(2, count + 1)]
    rest, given = total - most - (count - 1), [1] * (count - 1)
    while rest > 0:
        candidates = [i for i in range(count - 1) if given[i] < most]
        pool, remaining = sum([weights[i] for i in candidates]), rest
        for i in candidates:
            more = min(most - given[i], max(1, remaining * weights[i] // pool), rest)
            given[i] = given[i] + more
            rest = rest - more
    return np.array([most] + given)


def uneven_parts(own_key, count, total, bound, slope):
    if count == 2:
        one = jax.random.randint(own_key, (), max(1, total - bound), min(bound, total - 1) + 1)
        return jnp.stack([one, total - one])
    lengths = jnp.asarray(split_up(count, total, bound, slope), jnp.int32)
    twos = (count - 1) // 2
    giver, receiver = lengths[1:1 + 2 * twos:2], lengths[2:2 + 2 * twos:2]
    slack = jnp.minimum(giver - 1, bound - receiver)
    shifted = jax.random.randint(jax.random.fold_in(own_key, 1), (twos,), 0, 1 << 20) % (slack + 1)
    lengths = lengths.at[1:1 + 2 * twos:2].set(giver - shifted).at[2:2 + 2 * twos:2].set(receiver + shifted)
    return lengths[jax.random.permutation(jax.random.fold_in(own_key, 2), count)]


def bell_draw(rng, extent, spread, reach, cuts=(), kind=jnp.bfloat16):
    entries = jax.random.normal(rng, extent, jnp.float32) * spread
    if len(cuts) > 0:
        entries = levels(rng, extent, cuts, -0.22, 0.18) * entries
    return jnp.clip(entries, min=-reach, max=reach).astype(kind)


def setup_inputs(seed: int = 0, part: int = 0) -> dict:
    arg_keys = jax.random.split(jax.random.key(seed), 5)
    own_keys = jax.random.split(jax.random.fold_in(arg_keys[4], part), 5)
    return {
        "stored_query_rows": draw_stored_query_rows(jax.random.fold_in(jax.random.fold_in(arg_keys[4], part), 71), part),
        "stored_key_rows": draw_stored_key_rows(jax.random.fold_in(jax.random.fold_in(arg_keys[4], part), 71), part),
        "stored_value_rows": bell_draw(own_keys[2], (PACKED_TOKENS, KEY_VALUE_HEADS * HEAD_DIMENSION), 1.0, 6.0, ((0, 64),)),
        "block_docs": jnp.searchsorted(jnp.cumsum(uneven_parts(own_keys[3], DOCS, NBLOCKS, DOC_BLOCKS, 2)), jnp.arange(NBLOCKS), side="right").astype(jnp.int32),
    }


def reference(stored_query_rows, stored_key_rows, stored_value_rows, block_docs):
    query_group = QUERY_HEADS // KEY_VALUE_HEADS
    stored = jnp.arange(PACKED_TOKENS, dtype=jnp.int32)
    holder = stored // (2 * TOK_DEV)
    second = stored // TOK_DEV % 2
    piece_index = jnp.where(second == 0, holder, 2 * N_BLK - 1 - holder)
    position = (piece_index * TOK_DEV + stored % TOK_DEV).astype(jnp.int32)
    docs = block_docs[position // MASK_BLOCK_SIZE]
    expanded_keys = stored_key_rows.astype(jnp.float32).reshape(PACKED_TOKENS, KEY_VALUE_HEADS, HEAD_DIMENSION)
    expanded_values = stored_value_rows.astype(jnp.float32).reshape(PACKED_TOKENS, KEY_VALUE_HEADS, HEAD_DIMENSION)
    scale = 1.0 / math.sqrt(HEAD_DIMENSION)

    def one_block(index):
        first_token = (index * MASK_BLOCK_SIZE).astype(jnp.int32)
        query_block_rows = lax.dynamic_slice_in_dim(stored_query_rows, first_token, MASK_BLOCK_SIZE, 0).astype(jnp.float32).reshape(MASK_BLOCK_SIZE, KEY_VALUE_HEADS, query_group, HEAD_DIMENSION)
        query_pos = lax.dynamic_slice_in_dim(position, first_token, MASK_BLOCK_SIZE, 0)
        query_doc = lax.dynamic_slice_in_dim(docs, first_token, MASK_BLOCK_SIZE, 0)
        score = jnp.einsum('qhgd,khd->hgqk', query_block_rows, expanded_keys) * scale
        allowed = (docs[None, :] == query_doc[:, None]) & (position[None, :] <= query_pos[:, None])
        score = jnp.where(allowed, score, -1e+30)
        top = lax.optimization_barrier(jnp.max(score, axis=-1, keepdims=True))
        weight = jnp.where(allowed, jnp.exp(score - top), 0.0)
        total = lax.optimization_barrier(jnp.sum(weight, axis=-1))
        weight_low = lax.optimization_barrier(weight.astype(jnp.bfloat16)).astype(jnp.float32)
        summed = jnp.einsum('hgqk,khd->qhgd', weight_low, expanded_values)
        result = summed / jnp.moveaxis(total, 2, 0)[..., None]
        return result.reshape(MASK_BLOCK_SIZE, QUERY_HEADS * HEAD_DIMENSION).astype(jnp.bfloat16)
    blocks_out = lax.map(one_block, jnp.arange(PACKED_TOKENS // MASK_BLOCK_SIZE, dtype=jnp.int32))
    return blocks_out.reshape(PACKED_TOKENS, QUERY_HEADS * HEAD_DIMENSION)
```

```python
import functools
import math

import jax
import jax.numpy as jnp
from jax import lax
from jax.experimental import pallas as pl
from jax.experimental.pallas import tpu as pltpu
from jax.sharding import PartitionSpec as P

D = 128
T = 128
MESH = pl.DeviceIdType.MESH

HOPS = (
    ((1, 0, 0, 1, 3, 1), (1, 0, 0, 3, 1, -1), (1, 1, 0, 2, 3, 1), (1, 2, 0, 3, 3, 1),
     (1, 1, 0, 1, 4, 0), (1, 2, 0, 2, 4, 0), (1, 3, 0, 3, 4, 0), (2, 3, 1, 2, 2, -1),
     (2, 2, 3, 3, 2, 1), (2, 1, 3, 1, 7, 0), (2, 3, 1, 3, 5, 0), (2, 1, 4, 0, 5, -1),
     (2, 1, 4, 2, 7, 1), (2, 2, 4, 1, 5, -1), (2, 3, 3, 3, 7, 0), (2, 3, 4, 0, 7, 1),
     (2, 3, 4, 2, 5, -1), (3, 0, 5, 0, 1, 0), (3, 1, 5, 1, 1, 0), (3, 0, 7, 0, 3, 0),
     (3, 2, 5, 2, 1, 0), (3, 1, 7, 0, 4, -1), (3, 1, 7, 2, 6, 1), (3, 0, 5, 3, 6, -1),
     (3, 3, 7, 0, 6, 1), (3, 0, 7, 1, 6, 1), (4, 1, 1, 0, 2, -1), (4, 2, 1, 1, 2, -1)),
    ((1, 0, 0, 1, 3, 1), (1, 0, 0, 3, 1, -1), (1, 1, 0, 2, 3, 1), (1, 2, 0, 3, 3, 1),
     (1, 0, 0, 0, 4, 0), (1, 1, 0, 1, 4, 0), (1, 2, 0, 2, 4, 0), (1, 3, 0, 3, 4, 0),
     (2, 3, 1, 2, 2, -1), (2, 2, 3, 3, 2, 1), (2, 0, 4, 1, 7, 1), (2, 0, 4, 3, 5, -1),
     (2, 1, 4, 0, 5, -1), (2, 1, 4, 2, 7, 1), (2, 2, 4, 1, 5, -1), (2, 3, 3, 3, 7, 0),
     (2, 3, 4, 0, 7, 1), (2, 3, 4, 2, 5, -1), (3, 0, 5, 0, 1, 0), (3, 1, 5, 1, 1, 0),
     (3, 0, 7, 0, 3, 0), (3, 2, 5, 2, 1, 0), (3, 2, 2, 2, 6, 0), (3, 2, 7, 3, 6, 1),
     (3, 3, 7, 0, 6, 1), (3, 0, 7, 1, 6, 1), (4, 1, 1, 0, 2, -1), (4, 2, 1, 1, 2, -1)),
)
DEPTH = 4
MAX_OUT = 9


def tables():
    arrive = [[[] for _ in range(4)] for _ in HOPS]
    send = [[{} for _ in range(4)] for _ in HOPS]
    for u, hops in enumerate(HOPS):
        count = [0] * 4
        for depth, src, s_slot, dst, d_slot, move in hops:
            arrive[u][dst].append((depth, d_slot))
            send[u][src].setdefault(s_slot, []).append((d_slot, move, count[src]))
            count[src] += 1
    return arrive, send


ARRIVE, SEND = tables()


def kernel(heads, group, blk_count,
           docs, q_hbm, k_hbm, v_hbm, o_hbm,
           window, q_all, o_all, bias,
           own_sem, q_sem, o_sem, send_sem, recv_sem):
    blk, half = lax.axis_index("blk"), lax.axis_index("head")
    blocks = 2 * blk_count
    rows = blocks // 4
    me = jnp.where(half == 0, blk, blocks - 1 - blk)
    r, j = me // 4, lax.rem(me, 4)

    def device(row, col):
        at = 4 * lax.rem(row + rows, rows) + lax.rem(col + 4, 4)
        early = at < blk_count
        return {"blk": jnp.where(early, at, blocks - 1 - at), "head": jnp.where(early, 0, 1)}

    to = {0: device(r + 1, j), 1: device(r, j + 1), -1: device(r, j - 1)}

    def own_copy(u, h):
        cols = pl.ds(pl.multiple_of(h * D, D), D)
        return pltpu.make_async_copy(
            (k_hbm, v_hbm)[u].at[:, cols], window.at[u, h, 0], own_sem.at[u, h])

    def q_copy(n, h):
        cols = pl.ds(pl.multiple_of(n * D, D), D)
        return pltpu.make_async_copy(q_hbm.at[:, cols], q_all.at[n], q_sem.at[h])

    def o_copy(n, h):
        cols = pl.ds(pl.multiple_of(n * D, D), D)
        return pltpu.make_async_copy(o_all.at[n], o_hbm.at[:, cols], o_sem.at[h])

    def hop(u, h, s_slot, d_slot, move, number):
        return pltpu.make_async_remote_copy(
            src_ref=window.at[u, h, s_slot], dst_ref=window.at[u, h, d_slot],
            send_sem=send_sem.at[u, h, number], recv_sem=recv_sem.at[u, h, d_slot],
            device_id=to[move], device_id_type=MESH)

    @pl.loop(0, heads)
    def _(h):
        for u in range(2):
            own_copy(u, h).start()

    barrier = pltpu.get_barrier_semaphore()
    for there in (to[0], to[1], to[-1], device(r - 1, j)):
        pl.semaphore_signal(barrier, inc=1, device_id=there, device_id_type=MESH)

    my_doc = docs[me]
    for slot in range(8):
        col = lax.rem(j + slot, 4)
        if slot < 4:
            at = 4 * r + col - jnp.where(col > j, 8, 0)
        else:
            at = 4 * r - 4 + col
        same = (at >= 0) & (docs[jnp.maximum(at, 0)] == my_doc)
        bias[:, slot * T:(slot + 1) * T] = jnp.full(
            (8, T), jnp.where(same, 0.0, -jnp.inf), jnp.float32)

    pl.semaphore_wait(barrier, 4)

    scale = 1.0 / math.sqrt(D)

    def attend(h, part, parts):
        count = group // parts
        first = h * group + part * count
        key = window[0, h].reshape(8 * T, D)
        value = window[1, h].reshape(8 * T, D)
        row = lax.broadcasted_iota(jnp.int32, (1, T, T), 1)
        column = lax.broadcasted_iota(jnp.int32, (1, T, T), 2)
        causal = jnp.broadcast_to(column <= row, (count, T, T)).reshape(count * T, T)
        query = q_all[pl.ds(first, count)].reshape(count * T, D)
        score = lax.dot_general(query, key, (((1,), (1,)), ((), ())),
                                preferred_element_type=jnp.float32)
        own = jnp.where(causal, score[:, :T], -jnp.inf)
        rest = score[:, T:] + bias[0:1, T:]
        top = jnp.maximum(jnp.max(own, axis=1, keepdims=True),
                          jnp.max(rest, axis=1, keepdims=True))
        weight = jnp.concatenate(
            [jnp.exp((own - top) * scale), jnp.exp((rest - top) * scale)], axis=1)
        total = jnp.sum(weight, axis=1, keepdims=True)
        summed = jnp.dot(weight.astype(jnp.bfloat16), value, preferred_element_type=jnp.float32)
        out = (summed / total).astype(jnp.bfloat16)
        o_all[pl.ds(first, count)] = out.reshape(count, T, D)

    @pl.loop(0, heads + DEPTH + 1)
    def _(i):
        @pl.when(i < heads)
        def _():
            @pl.loop(0, group)
            def _(g):
                q_copy(i * group + g, i).start()
            for u in range(2):
                own_copy(u, i).wait()

        done = i - DEPTH - 1
        for u in range(2):
            for col in range(4):
                @pl.when(j == col)
                def _(u=u, col=col):
                    for depth in range(DEPTH, -1, -1):
                        h = i - depth
                        slots = ([0] if depth == 0 else
                                 [s for d, s in ARRIVE[u][col] if d == depth])
                        if not slots:
                            continue

                        @pl.when((h >= 0) & (h < heads))
                        def _(h=h, slots=slots, depth=depth):
                            for slot in slots:
                                if depth:
                                    hop(u, h, slot, slot, 1, 0).wait_recv()
                                for d_slot, move, number in SEND[u][col].get(slot, ()):
                                    hop(u, h, slot, d_slot, move, number).start()

            @pl.when(done >= 0)
            def _(u=u):
                if u == 0:
                    pltpu.make_async_copy(
                        o_all.at[pl.ds(done * group, group)],
                        q_all.at[pl.ds(done * group, group)], q_sem.at[done]).wait()
                attend(done, u, 2)

                @pl.loop(0, group // 2)
                def _(g):
                    o_copy(done * group + u * (group // 2) + g, done).start()

    @pl.loop(0, heads)
    def _(h):
        pltpu.make_async_copy(
            q_all.at[pl.ds(h * group, group)],
            o_all.at[pl.ds(h * group, group)], o_sem.at[h]).wait()
        for u in range(2):
            for col in range(4):
                @pl.when(j == col)
                def _(u=u, col=col):
                    for slot, outs in SEND[u][col].items():
                        for d_slot, move, number in outs:
                            hop(u, h, slot, d_slot, move, number).wait_send()


def on_device(queries, keys, values, block_docs):
    blk_count = lax.axis_size("blk")
    heads = keys.shape[1] // D
    group = queries.shape[1] // keys.shape[1]
    anywhere = pl.BlockSpec(memory_space=pl.ANY)
    return pl.pallas_call(
        functools.partial(kernel, heads, group, blk_count),
        out_shape=jax.ShapeDtypeStruct(queries.shape, jnp.bfloat16),
        in_specs=[pl.BlockSpec(memory_space=pltpu.SMEM), anywhere, anywhere, anywhere],
        out_specs=anywhere,
        scratch_shapes=[
            pltpu.VMEM((2, heads, 8, T, D), jnp.bfloat16),
            pltpu.VMEM((heads * group, T, D), jnp.bfloat16),
            pltpu.VMEM((heads * group, T, D), jnp.bfloat16),
            pltpu.VMEM((8, 8 * T), jnp.float32),
            pltpu.SemaphoreType.DMA((2, heads)),
            pltpu.SemaphoreType.DMA((heads,)),
            pltpu.SemaphoreType.DMA((heads,)),
            pltpu.SemaphoreType.DMA((2, heads, MAX_OUT)),
            pltpu.SemaphoreType.DMA((2, heads, 8)),
        ],
        compiler_params=pltpu.CompilerParams(
            collective_id=0, has_side_effects=True, vmem_limit_bytes=48 << 20),
        name="window_attention",
    )(block_docs, queries, keys, values)


def solution(mesh):
    rows = P(("dp", "blk", "head"), None)
    return jax.shard_map(
        on_device, mesh=mesh, in_specs=(rows, rows, rows, P("dp")), out_specs=rows,
        check_vma=False)
```

```python
import functools
import math

import jax
import jax.numpy as jnp
from jax import lax
from jax.experimental import pallas as pl
from jax.experimental.pallas import tpu as pltpu
from jax.sharding import PartitionSpec as P

D = 128
T = 128
BLOCKS = 64
SPAN = 8
MESH = pl.DeviceIdType.MESH

TREES = (
    (1, 3, 194, 4, 69, 263, 454,),
    (64, 66, 131, 69, 324, 134, 199, 12, 776,),
    (131, 134, 389, 324, 263, 329, 584,),
    (199, 452, 454, 389, 264, 394, 649,),
    (261, 326, 264, 521, 523, 711, 425, 2661, 2378,),
    (326, 391, 329, 584, 586, 459, 524,),
    (386, 129, 391, 394, 649, 77, 844, 488, 2596, 2315, 712,),
    (451, 192, 459, 712, 714, 12, 781, 841, 693, 3441, 3150,),
    (521, 523, 714, 524, 589, 846, 756, 3376, 3087,),
    (586, 651, 589, 844, 654, 783, 819, 3327, 4048,),
    (651, 654, 909, 719, 972, 882, 3262, 3985, 1104,),
    (719, 972, 974, 909, 929, 2157, 2898, 819, 3292, 1808, 1041,),
    (781, 783, 974, 803, 2287, 3024, 1041, 1106, 1043,),
    (846, 911, 866, 2222, 2961, 1104, 1106, 1171, 1044,),
    (898, 911, 992, 2092, 2835, 1232, 189, 3922, 1169, 1109, 1364,),
    (1008, 3103, 2003, 1232, 1234, 1169, 1044, 1301, 1174,),
    (1043, 1234, 1239, 1492, 1494, 1429, 1361,),
    (1109, 1364, 1366, 1426, 1303, 1491, 1304,),
    (1171, 1174, 1429, 1369, 1624, 1556, 1276, 3896, 3607,),
    (1239, 1492, 1494, 1434, 1689, 1621, 1323, 2791, 2520,),
    (1301, 1303, 1304, 1561, 1499, 1754, 1686,),
    (1366, 1431, 1369, 1624, 1626, 1563, 1564,),
    (1431, 1434, 1689, 1629, 1884, 1816, 1823, 2011,),
    (1499, 1752, 1754, 1564, 1694, 1949, 1881,),
    (1561, 1563, 1759, 2014, 1946, 1591, 3571, 3292, 1821,),
    (1626, 1691, 1629, 1884, 1886, 1823, 2016,),
    (1691, 1694, 1949, 1951, 2012, 1953, 2144,),
    (1759, 2012, 1821, 2014, 2016, 2081, 1890,),
    (1827, 2272, 2079, 2274, 2205, 2209, 2142,),
    (1890, 2209, 2142, 2211, 2272, 2079, 2084,),
    (1946, 1951, 1953, 2144, 2146, 2083, 1701, 2404,),
    (2011, 1764, 2336, 2083, 2341, 2401, 2406, 2466,),
    (2081, 2084, 2149, 2343, 2531, 2274, 2534,),
    (2146, 2211, 2149, 2404, 2331, 1751, 2214, 2279, 1512,),
    (2214, 2469, 2471, 2531, 2532, 2409, 2664,),
    (2279, 2532, 2534, 2469, 2344, 2474, 2729,),
    (2341, 2406, 2343, 2504, 516, 2344, 2601, 299, 2794,),
    (2409, 2664, 2666, 2726, 2603, 2791, 2604,),
    (2471, 2474, 2729, 2539, 2792, 2567, 451, 236, 2669,),
    (2539, 2792, 2601, 2794, 2604, 2734, 2989,),
    (2583, 1491, 2603, 2772, 1296, 1260, 2861, 2921, 1071, 3054, 2986,),
    (2666, 2693, 321, 2731, 2669, 2924, 2848, 2063, 110, 2863, 1008,),
    (2731, 2734, 2989, 2913, 2126, 2799, 3052, 945, 3184,),
    (2799, 3052, 2819, 194, 173, 3054, 2978, 2205, 1886, 1969, 1906, 252, 3888,),
    (2835, 1247, 2861, 2926, 2863, 2032, 3121, 3123, 3314,),
    (2882, 142, 2926, 2991, 3008, 945, 3184, 3186, 3124, 63, 4083,),
    (2945, 2991, 126, 4018, 3249, 3251, 3312, 3189, 3444,),
    (3043, 2268, 1843, 3312, 3314, 3249, 3124, 3381, 3254,),
    (3121, 3123, 3189, 3444, 3446, 3506, 3319,),
    (3186, 3251, 3197, 3961, 3701, 3446, 3704, 3636, 3383,),
    (3254, 3509, 3511, 3571, 3572, 3339, 711, 504, 3449,),
    (3319, 3572, 3574, 3509, 3384, 3514, 3769,),
    (3381, 3418, 1686, 3383, 3574, 3384, 1465, 3643, 3834,),
    (3449, 3704, 3706, 3766, 3643, 3831, 3644,),
    (3511, 3514, 3769, 3579, 3832, 3709, 3964,),
    (3579, 3832, 3641, 3834, 3644, 3709, 3774,),
    (3636, 3376, 3641, 3132, 3901, 3903, 4091, 4094, 4026,),
    (3670, 1426, 3706, 3733, 1361, 3771, 3796, 1296, 1213, 3964, 1150, 1087,),
    (3771, 3774, 4029, 3839, 4092,),
    (3839, 4092, 4094, 4029,),
    (3901, 3966, 3903,),
    (3966, 4031,),
    (4031,),
)


def programs():
    arrive = [{} for _ in range(BLOCKS)]
    send = [{} for _ in range(BLOCKS)]
    extra = [SPAN] * BLOCKS
    count = [0] * BLOCKS
    for block, hops in enumerate(TREES):
        slot, depth = {block: 0}, {block: 0}
        for hop in hops:
            src, dst = hop // BLOCKS, hop % BLOCKS
            depth[dst] = depth[src] + 1
            if 0 < dst - block < SPAN:
                slot[dst] = dst - block
            else:
                slot[dst] = extra[dst]
                extra[dst] += 1
            arrive[dst].setdefault(depth[dst], []).append(slot[dst])
            send[src].setdefault(slot[src], []).append((dst, slot[dst], count[src]))
            count[src] += 1
    deepest = max(max(a) for a in arrive if a)
    return arrive, send, max(extra), max(count), deepest


ARRIVE, SEND, SLOTS, MAX_OUT, DEPTH = programs()
PARTS = 4
OFFSET = tuple(2 * d for d in range(DEPTH + 1))


def kernel(heads, group, blk_count,
           docs, q_hbm, k_hbm, v_hbm, o_hbm,
           window, q_all, o_all, bias,
           own_sem, q_sem, o_sem, send_sem, recv_sem):
    blk, half = lax.axis_index("blk"), lax.axis_index("head")
    me = jnp.where(half == 0, blk, BLOCKS - 1 - blk)
    z_hi, x, y = blk // 16, lax.rem(blk // 4, 4), lax.rem(blk, 4)

    def own_copy(u, h):
        cols = pl.ds(pl.multiple_of(h * D, D), D)
        return pltpu.make_async_copy(
            (k_hbm, v_hbm)[u].at[:, cols], window.at[h, 0, u], own_sem.at[u, h])

    def q_copy(n, h):
        cols = pl.ds(pl.multiple_of(n * D, D), D)
        return pltpu.make_async_copy(q_hbm.at[:, cols], q_all.at[n], q_sem.at[h])

    def o_copy(n, h):
        cols = pl.ds(pl.multiple_of(n * D, D), D)
        return pltpu.make_async_copy(o_all.at[n], o_hbm.at[:, cols], o_sem.at[h])

    def hop(h, s_slot, d_slot, there, number):
        early = there < BLOCKS // 2
        return pltpu.make_async_remote_copy(
            src_ref=window.at[h, s_slot], dst_ref=window.at[h, d_slot],
            send_sem=send_sem.at[h, number], recv_sem=recv_sem.at[h, d_slot],
            device_id={"blk": there if early else BLOCKS - 1 - there, "head": 0 if early else 1},
            device_id_type=MESH)

    def on_block(body, low=0, high=BLOCKS):
        if high - low == 1:
            return body(low)
        mid = (low + high) // 2

        @pl.when(me < mid)
        def _():
            on_block(body, low, mid)

        @pl.when(me >= mid)
        def _():
            on_block(body, mid, high)

    @pl.loop(0, heads)
    def _(h):
        for u in range(2):
            own_copy(u, h).start()

    barrier = pltpu.get_barrier_semaphore()
    for dx, dy, dz in ((1, 0, 0), (3, 0, 0), (0, 1, 0), (0, 3, 0), (0, 0, 1), (0, 0, 3)):
        z = lax.rem(2 * z_hi + half + dz, 4)
        there = {"blk": z // 2 * 16 + lax.rem(x + dx, 4) * 4 + lax.rem(y + dy, 4),
                 "head": lax.rem(z, 2)}
        pl.semaphore_signal(barrier, inc=1, device_id=there, device_id_type=MESH)

    my_doc = docs[me]
    for slot in range(SPAN):
        at = me - slot
        same = (at >= 0) & (docs[jnp.maximum(at, 0)] == my_doc)
        bias[slot * T:(slot + 1) * T] = jnp.where(
            lax.broadcasted_iota(jnp.int32, (T, D), 1) == 0,
            jnp.where(same, 0.0, -1e30), 0.0).astype(jnp.bfloat16)

        @pl.when(at < 0)
        def _(slot=slot):
            @pl.loop(0, heads)
            def _(h):
                window[h, slot] = jnp.zeros((2, T, D), jnp.bfloat16)

    pl.semaphore_wait(barrier, 6)

    lane = lax.broadcasted_iota(jnp.int32, (1, D), 1)
    factor = math.log2(math.e) / math.sqrt(D)

    def attend(h, part, parts):
        count = group // parts
        first = h * group + part * count
        key = jnp.concatenate([window[h, :SPAN, 0].reshape(SPAN * T, D), bias[...]], axis=1)
        value = jnp.concatenate(
            [window[h, :SPAN, 1].reshape(SPAN * T, D),
             jnp.ones((SPAN * T, D), jnp.bfloat16)], axis=1)
        marker = jnp.broadcast_to(jnp.where(lane == 0, 1.0, 0.0), (count * T, D))
        query = jnp.concatenate(
            [q_all[pl.ds(first, count)].reshape(count * T, D), marker.astype(jnp.bfloat16)], axis=1)
        row = lax.broadcasted_iota(jnp.int32, (1, T, T), 1)
        column = lax.broadcasted_iota(jnp.int32, (1, T, T), 2)
        causal = jnp.broadcast_to(column <= row, (count, T, T)).reshape(count * T, T)
        score = lax.dot_general(query, key, (((1,), (1,)), ((), ())),
                                preferred_element_type=jnp.float32)
        pieces = [jnp.where(causal, score[:, :T], -1e30)]
        pieces += [score[:, n * T:(n + 1) * T] for n in range(1, SPAN)]
        top = jnp.max(functools.reduce(jnp.maximum, pieces), axis=1, keepdims=True)
        weight = jnp.concatenate(
            [jnp.exp2((piece - top) * factor).astype(jnp.bfloat16) for piece in pieces], axis=1)
        summed = jnp.dot(weight, value, preferred_element_type=jnp.float32)
        out = (summed[:, :D] / summed[:, D:]).astype(jnp.bfloat16)
        o_all[pl.ds(first, count)] = out.reshape(count, T, D)

    @pl.loop(0, heads + OFFSET[DEPTH])
    def _(i):
        @pl.when(i < heads)
        def _():
            @pl.loop(0, group)
            def _(g):
                q_copy(i * group + g, i).start()
            for u in range(2):
                own_copy(u, i).wait()

        def travel(block):
            for depth in range(DEPTH, -1, -1):
                h = i - OFFSET[depth]
                slots = ARRIVE[block].get(depth, []) if depth else [0]
                if not slots:
                    continue

                @pl.when((h >= 0) & (h < heads))
                def _(h=h, slots=slots, depth=depth):
                    for slot in slots:
                        if depth:
                            hop(h, slot, slot, (block + 1) % BLOCKS, 0).wait_recv()
                        for there, d_slot, number in SEND[block].get(slot, ()):
                            hop(h, slot, d_slot, there, number).start()

        on_block(travel)
        done = i - OFFSET[DEPTH]

        @pl.when(done >= 0)
        def _():
            pltpu.make_async_copy(
                o_all.at[pl.ds(done * group, group)],
                q_all.at[pl.ds(done * group, group)], q_sem.at[done]).wait()
            for part in range(PARTS):
                attend(done, part, PARTS)

            @pl.loop(0, group)
            def _(g):
                o_copy(done * group + g, done).start()

    def finish(block):
        @pl.loop(0, heads)
        def _(h):
            for slot, outs in SEND[block].items():
                for there, d_slot, number in outs:
                    hop(h, slot, d_slot, there, number).wait_send()

    on_block(finish)

    @pl.loop(0, heads)
    def _(h):
        pltpu.make_async_copy(
            q_all.at[pl.ds(h * group, group)],
            o_all.at[pl.ds(h * group, group)], o_sem.at[h]).wait()


def on_device(queries, keys, values, block_docs):
    blk_count = lax.axis_size("blk")
    heads = keys.shape[1] // D
    group = queries.shape[1] // keys.shape[1]
    anywhere = pl.BlockSpec(memory_space=pltpu.HBM)
    return pl.pallas_call(
        functools.partial(kernel, heads, group, blk_count),
        out_shape=jax.ShapeDtypeStruct(queries.shape, jnp.bfloat16),
        in_specs=[pl.BlockSpec(memory_space=pltpu.SMEM), anywhere, anywhere, anywhere],
        out_specs=anywhere,
        scratch_shapes=[
            pltpu.VMEM((heads, SLOTS, 2, T, D), jnp.bfloat16),
            pltpu.VMEM((heads * group, T, D), jnp.bfloat16),
            pltpu.VMEM((heads * group, T, D), jnp.bfloat16),
            pltpu.VMEM((SPAN * T, D), jnp.bfloat16),
            pltpu.SemaphoreType.DMA((2, heads)),
            pltpu.SemaphoreType.DMA((heads,)),
            pltpu.SemaphoreType.DMA((heads,)),
            pltpu.SemaphoreType.DMA((heads, MAX_OUT)),
            pltpu.SemaphoreType.DMA((heads, SLOTS)),
        ],
        compiler_params=pltpu.CompilerParams(
            collective_id=0, has_side_effects=True, vmem_limit_bytes=62 << 20),
        name="window_attention",
    )(block_docs, queries, keys, values)


def solution(mesh):
    rows = P(("dp", "blk", "head"), None)
    return jax.shard_map(
        on_device, mesh=mesh, in_specs=(rows, rows, rows, P("dp")), out_specs=rows,
        check_vma=False)
```

```python
import functools
import math

import jax
import jax.numpy as jnp
from jax import lax
from jax.experimental import pallas as pl
from jax.experimental.pallas import tpu as pltpu
from jax.sharding import PartitionSpec as P

D = 128
T = 128
BLOCKS = 64
SPAN = 8
MESH = pl.DeviceIdType.MESH

TREES = (
    (1, 3, 194, 4, 69, 263, 454,),
    (66, 131, 69, 324, 134, 299, 2791, 2504, 236, 2856, 2567,),
    (131, 134, 389, 324, 199, 329, 584,),
    (199, 452, 261, 454, 264, 394, 649,),
    (261, 326, 263, 264, 521, 523, 714,),
    (321, 64, 326, 391, 329, 586, 459, 712, 12,),
    (391, 394, 649, 584, 651, 589, 844,),
    (459, 712, 521, 714, 524, 654, 909,),
    (523, 524, 781, 841, 719, 974, 906,),
    (586, 589, 844, 768, 783, 971, 16, 693, 3441, 3150,),
    (651, 711, 451, 192, 12, 654, 909, 833, 207, 16, 81,),
    (719, 972, 974, 898, 129, 77, 81, 146, 803, 2268, 1808,),
    (781, 846, 783, 796, 1808, 1041, 1106, 992, 2092, 2835,),
    (846, 911, 861, 1873, 1104, 1106, 1043, 1044,),
    (911, 963, 211, 1232, 926, 1938, 1169, 1949, 1881, 1621, 1364,),
    (991, 2003, 1232, 1234, 1169, 1044, 1301, 1174,),
    (1041, 1043, 1234, 1109, 1239, 1492, 1494,),
    (1104, 1109, 1366, 1426, 1171, 1052, 1816, 1556, 1303,),
    (1171, 1174, 1429, 1364, 1431, 1304, 1561,),
    (1239, 1492, 1494, 1429, 1304, 1369, 1434,),
    (1301, 1303, 1499, 1752, 1754, 1686, 1386, 2726, 2457,),
    (1366, 1369, 1624, 1563, 1751, 1564, 1449, 2661, 2394,),
    (1431, 1491, 1434, 1689, 1624, 1247, 2012, 1821, 1528, 3636, 3355,),
    (1499, 1752, 1754, 1689, 1564, 1629, 1694,),
    (1561, 1626, 1563, 1759, 2014, 1654, 3506, 3229, 1591, 3571, 3292,),
    (1626, 1691, 1629, 1884, 1886, 1823, 1827, 2272,),
    (1691, 1694, 1949, 1884, 1759, 2016, 1701, 2401,),
    (1764, 2336, 2079, 2012, 2081, 2142, 2146, 2205,),
    (1821, 1823, 2014, 1953, 1890, 1827, 2272,),
    (1886, 1951, 1890, 2209, 2144, 2211, 2084,),
    (1946, 1951, 1953, 2144, 2146, 2083, 1701, 2404,),
    (2011, 2016, 2083, 2274, 2209, 1764, 2341, 2214,),
    (2081, 2084, 2149, 2343, 2531, 2274, 2534,),
    (2149, 2404, 2331, 1751, 2406, 2466, 2343, 2531, 1512,),
    (2211, 2214, 2469, 2378, 646, 2279, 2532, 2344, 425,),
    (2279, 2532, 2534, 2469, 2474, 2729, 2664,),
    (2341, 2344, 2409, 2666, 2726, 2603, 2791,),
    (2406, 2471, 2409, 2664, 2603, 2794, 2604,),
    (2471, 2474, 2729, 2539, 2792, 2669, 2924,),
    (2539, 2792, 2583, 1491, 2601, 2794, 1260, 2734, 2989,),
    (2601, 2630, 386, 389, 321, 362, 2604, 173, 110, 2863, 3051,),
    (2666, 2731, 2772, 1296, 2669, 2924, 2848, 2063, 2926, 1071, 1008,),
    (2731, 2734, 2989, 2799, 3052, 2941, 3953, 3184,),
    (2799, 3052, 2861, 3054, 2876, 3888, 3006, 4018, 3249,),
    (2848, 2861, 2863, 3054, 2096, 3121, 3123, 3314,),
    (2913, 2926, 2991, 3043, 2161, 3184, 3186, 2291, 3124,),
    (2978, 2991, 2226, 3249, 3251, 3312, 3189, 3444,),
    (3071, 4083, 3312, 3121, 3314, 3124, 3381, 3254,),
    (3087, 971, 3123, 756, 3319, 3574, 3506, 3509, 3441,),
    (3186, 3189, 3444, 3339, 711, 3446, 3383, 3571, 504,),
    (3251, 3254, 3509, 3418, 1686, 3319, 3572, 3384, 1465,),
    (3327, 4091, 3831, 3572, 3574, 3832, 3641, 3701, 3514,),
    (3381, 3383, 3384, 3449, 3643, 3834, 3766,),
    (3446, 3465, 581, 3511, 3449, 3704, 3636, 3376, 378, 3579, 3132,),
    (3511, 3528, 516, 3514, 3769, 3704, 315, 3644, 3709,),
    (3579, 3832, 3834, 3769, 3644, 3901, 3774,),
    (3641, 3706, 3643, 3709, 3964, 3774, 3839,),
    (3670, 1426, 3706, 3771, 1213, 3964, 3966, 3903,),
    (3733, 1361, 3771, 3796, 1296, 1150, 4029, 1087, 4092,),
    (3839, 4092, 4094, 4029,),
    (3901, 3903, 4094,),
    (3966, 4031,),
    (4031,),
)


def programs():
    arrive = [{} for _ in range(BLOCKS)]
    send = [{} for _ in range(BLOCKS)]
    extra = [SPAN] * BLOCKS
    count = [0] * BLOCKS
    for block, hops in enumerate(TREES):
        slot, depth = {block: 0}, {block: 0}
        for hop in hops:
            src, dst = hop // BLOCKS, hop % BLOCKS
            depth[dst] = depth[src] + 1
            if 0 < dst - block < SPAN:
                slot[dst] = dst - block
            else:
                slot[dst] = extra[dst]
                extra[dst] += 1
            arrive[dst].setdefault(depth[dst], []).append(slot[dst])
            send[src].setdefault(slot[src], []).append((dst, slot[dst], depth[dst]))
            count[src] += 1
    deepest = max(max(a) for a in arrive if a)
    return arrive, send, max(extra), count, deepest


ARRIVE, SEND, SLOTS, SENDS, DEPTH = programs()
PARTS = 4
OFFSET = tuple(2 * d for d in range(DEPTH + 1))


def kernel(heads, group, blk_count,
           docs, q_hbm, k_hbm, v_hbm, o_hbm,
           window, q_all, o_all, bias,
           own_sem, q_sem, o_sem, send_sem, recv_sem):
    blk, half = lax.axis_index("blk"), lax.axis_index("head")
    me = jnp.where(half == 0, blk, BLOCKS - 1 - blk)
    z_hi, x, y = blk // 16, lax.rem(blk // 4, 4), lax.rem(blk, 4)

    def own_copy(u, h):
        cols = pl.ds(pl.multiple_of(h * D, D), D)
        return pltpu.make_async_copy(
            (k_hbm, v_hbm)[u].at[:, cols], window.at[h, 0, u], own_sem.at[u, h])

    def q_copy(h):
        cols = pl.ds(pl.multiple_of(h * group * D, group * D), group * D)
        return pltpu.make_async_copy(q_hbm.at[:, cols], q_all.at[h], q_sem.at[h])

    def o_copy(h):
        cols = pl.ds(pl.multiple_of(h * group * D, group * D), group * D)
        return pltpu.make_async_copy(o_all.at[h], o_hbm.at[:, cols], o_sem.at[h])

    def hop(h, s_slot, d_slot, there, depth):
        early = there < BLOCKS // 2
        return pltpu.make_async_remote_copy(
            src_ref=window.at[h, s_slot], dst_ref=window.at[h, d_slot],
            send_sem=send_sem.at[0], recv_sem=recv_sem.at[h, depth - 1],
            device_id={"blk": there if early else BLOCKS - 1 - there, "head": 0 if early else 1},
            device_id_type=MESH)

    def wait_bytes(ref, sem):
        pltpu.make_async_copy(ref, ref, sem).wait()

    def on_block(body, low=0, high=BLOCKS):
        if high - low == 1:
            return body(low)
        mid = (low + high) // 2

        @pl.when(me < mid)
        def _():
            on_block(body, low, mid)

        @pl.when(me >= mid)
        def _():
            on_block(body, mid, high)

    barrier = pltpu.get_barrier_semaphore()
    for dx, dy, dz in [tuple(hops * (axis == at) for at in range(3))
                       for axis in range(3) for hops in (1, 2, 3)]:
        z = lax.rem(2 * z_hi + half + dz, 4)
        there = {"blk": z // 2 * 16 + lax.rem(x + dx, 4) * 4 + lax.rem(y + dy, 4),
                 "head": lax.rem(z, 2)}
        pl.semaphore_signal(barrier, inc=1, device_id=there, device_id_type=MESH)

    @pl.loop(0, heads)
    def _(h):
        for u in range(2):
            own_copy(u, h).start()

    my_doc = docs[me]
    for slot in range(SPAN):
        at = me - slot
        same = (at >= 0) & (docs[jnp.maximum(at, 0)] == my_doc)
        bias[slot * T:(slot + 1) * T] = jnp.where(
            lax.broadcasted_iota(jnp.int32, (T, D), 1) == 0,
            jnp.where(same, 0.0, -1e30), 0.0).astype(jnp.bfloat16)

        @pl.when(at < 0)
        def _(slot=slot):
            @pl.loop(0, heads)
            def _(h):
                window[h, slot] = jnp.zeros((2, T, D), jnp.bfloat16)

    pl.semaphore_wait(barrier, 9)

    lane = lax.broadcasted_iota(jnp.int32, (1, D), 1)
    factor = math.log2(math.e) / math.sqrt(D)

    def attend(h, part, parts):
        count = group // parts
        first = part * count
        key = jnp.concatenate([window[h, :SPAN, 0].reshape(SPAN * T, D), bias[...]], axis=1)
        value = jnp.concatenate(
            [window[h, :SPAN, 1].reshape(SPAN * T, D),
             jnp.ones((SPAN * T, D), jnp.bfloat16)], axis=1)
        marker = jnp.broadcast_to(jnp.where(lane == 0, 1.0, 0.0), (count * T, D))
        query = jnp.concatenate(
            [jnp.concatenate([q_all[h, :, (first + g) * D:(first + g + 1) * D]
                              for g in range(count)], axis=0), marker.astype(jnp.bfloat16)], axis=1)
        row = lax.broadcasted_iota(jnp.int32, (1, T, T), 1)
        column = lax.broadcasted_iota(jnp.int32, (1, T, T), 2)
        causal = jnp.broadcast_to(column <= row, (count, T, T)).reshape(count * T, T)
        score = lax.dot_general(query, key, (((1,), (1,)), ((), ())),
                                preferred_element_type=jnp.float32)
        pieces = [jnp.where(causal, score[:, :T], -1e30)]
        pieces += [score[:, n * T:(n + 1) * T] for n in range(1, SPAN)]
        top = jnp.max(functools.reduce(jnp.maximum, pieces), axis=1, keepdims=True)
        weight = jnp.concatenate(
            [jnp.exp2((piece - top) * factor).astype(jnp.bfloat16) for piece in pieces], axis=1)
        summed = jnp.dot(weight, value, preferred_element_type=jnp.float32)
        out = (summed[:, :D] / summed[:, D:]).astype(jnp.bfloat16)
        for g in range(count):
            o_all[h, :, (first + g) * D:(first + g + 1) * D] = out[g * T:(g + 1) * T]

    @pl.loop(0, heads + OFFSET[DEPTH])
    def _(i):
        @pl.when(i < heads)
        def _():
            q_copy(i).start()
            for u in range(2):
                own_copy(u, i).wait()

        def travel(block):
            for depth in range(DEPTH, -1, -1):
                h = i - OFFSET[depth]
                slots = ARRIVE[block].get(depth, []) if depth else [0]
                if not slots:
                    continue

                @pl.when((h >= 0) & (h < heads))
                def _(h=h, slots=slots, depth=depth):
                    if depth:
                        wait_bytes(window.at[h, pl.ds(0, len(slots))], recv_sem.at[h, depth - 1])
                    for slot in slots:
                        for there, d_slot, later in SEND[block].get(slot, ()):
                            hop(h, slot, d_slot, there, later).start()

        on_block(travel)
        done = i - OFFSET[DEPTH]

        @pl.when(done >= 0)
        def _():
            q_copy(done).wait()
            for part in range(PARTS):
                attend(done, part, PARTS)

            o_copy(done).start()

    def finish(block):
        if SENDS[block]:
            wait_bytes(window.at[:, pl.ds(0, SENDS[block])], send_sem.at[0])

    on_block(finish)

    @pl.loop(0, heads)
    def _(h):
        o_copy(h).wait()


def on_device(queries, keys, values, block_docs):
    blk_count = lax.axis_size("blk")
    heads = keys.shape[1] // D
    group = queries.shape[1] // keys.shape[1]
    anywhere = pl.BlockSpec(memory_space=pltpu.HBM)
    return pl.pallas_call(
        functools.partial(kernel, heads, group, blk_count),
        out_shape=jax.ShapeDtypeStruct(queries.shape, jnp.bfloat16),
        in_specs=[pl.BlockSpec(memory_space=pltpu.SMEM), anywhere, anywhere, anywhere],
        out_specs=anywhere,
        scratch_shapes=[
            pltpu.VMEM((heads, SLOTS, 2, T, D), jnp.bfloat16),
            pltpu.VMEM((heads, T, group * D), jnp.bfloat16),
            pltpu.VMEM((heads, T, group * D), jnp.bfloat16),
            pltpu.VMEM((SPAN * T, D), jnp.bfloat16),
            pltpu.SemaphoreType.DMA((2, heads)),
            pltpu.SemaphoreType.DMA((heads,)),
            pltpu.SemaphoreType.DMA((heads,)),
            pltpu.SemaphoreType.DMA((1,)),
            pltpu.SemaphoreType.DMA((heads, DEPTH)),
        ],
        compiler_params=pltpu.CompilerParams(
            collective_id=0, has_side_effects=True, vmem_limit_bytes=62 << 20),
        name="window_attention",
    )(block_docs, queries, keys, values)


def solution(mesh):
    rows = P(("dp", "blk", "head"), None)
    return jax.shard_map(
        on_device, mesh=mesh, in_specs=(rows, rows, rows, P("dp")), out_specs=rows,
        check_vma=False)
```

```python
import functools
import math

import jax
import jax.numpy as jnp
from jax import lax
from jax.experimental import pallas as pl
from jax.experimental.pallas import tpu as pltpu
from jax.sharding import PartitionSpec as P

D = 128
T = 128
BLOCKS = 64
SPAN = 8
MESH = pl.DeviceIdType.MESH

TREES = (
    (1, 3, 194, 4, 69, 263, 454,),
    (66, 131, 69, 324, 134, 299, 2791, 2504, 236, 2856, 2567,),
    (131, 134, 389, 324, 199, 329, 584,),
    (199, 452, 261, 454, 264, 394, 649,),
    (261, 326, 263, 264, 521, 523, 714,),
    (321, 64, 326, 391, 329, 586, 459, 712, 12,),
    (391, 394, 649, 584, 651, 589, 844,),
    (459, 712, 521, 714, 524, 654, 909,),
    (523, 524, 781, 841, 719, 974, 906,),
    (586, 589, 844, 768, 783, 971, 16, 693, 3441, 3150,),
    (651, 711, 451, 192, 12, 654, 909, 833, 207, 16, 81,),
    (719, 972, 974, 898, 129, 77, 81, 146, 803, 2268, 1808,),
    (781, 846, 783, 796, 1808, 1041, 1106, 992, 2092, 2835,),
    (846, 911, 861, 1873, 1104, 1106, 1043, 1044,),
    (911, 963, 211, 1232, 926, 1938, 1169, 1949, 1881, 1621, 1364,),
    (991, 2003, 1232, 1234, 1169, 1044, 1301, 1174,),
    (1041, 1043, 1234, 1109, 1239, 1492, 1494,),
    (1104, 1109, 1366, 1426, 1171, 1052, 1816, 1556, 1303,),
    (1171, 1174, 1429, 1364, 1431, 1304, 1561,),
    (1239, 1492, 1494, 1429, 1304, 1369, 1434,),
    (1301, 1303, 1499, 1752, 1754, 1686, 1386, 2726, 2457,),
    (1366, 1369, 1624, 1563, 1751, 1564, 1449, 2661, 2394,),
    (1431, 1491, 1434, 1689, 1624, 1247, 2012, 1821, 1528, 3636, 3355,),
    (1499, 1752, 1754, 1689, 1564, 1629, 1694,),
    (1561, 1626, 1563, 1759, 2014, 1654, 3506, 3229, 1591, 3571, 3292,),
    (1626, 1691, 1629, 1884, 1886, 1823, 1827, 2272,),
    (1691, 1694, 1949, 1884, 1759, 2016, 1701, 2401,),
    (1764, 2336, 2079, 2012, 2081, 2142, 2146, 2205,),
    (1821, 1823, 2014, 1953, 1890, 1827, 2272,),
    (1886, 1951, 1890, 2209, 2144, 2211, 2084,),
    (1946, 1951, 1953, 2144, 2146, 2083, 1701, 2404,),
    (2011, 2016, 2083, 2274, 2209, 1764, 2341, 2214,),
    (2081, 2084, 2149, 2343, 2531, 2274, 2534,),
    (2149, 2404, 2331, 1751, 2406, 2466, 2343, 2531, 1512,),
    (2211, 2214, 2469, 2378, 646, 2279, 2532, 2344, 425,),
    (2279, 2532, 2534, 2469, 2474, 2729, 2664,),
    (2341, 2344, 2409, 2666, 2726, 2603, 2791,),
    (2406, 2471, 2409, 2664, 2603, 2794, 2604,),
    (2471, 2474, 2729, 2539, 2792, 2669, 2924,),
    (2539, 2792, 2583, 1491, 2601, 2794, 1260, 2734, 2989,),
    (2601, 2630, 386, 389, 321, 362, 2604, 173, 110, 2863, 3051,),
    (2666, 2731, 2772, 1296, 2669, 2924, 2848, 2063, 2926, 1071, 1008,),
    (2731, 2734, 2989, 2799, 3052, 2941, 3953, 3184,),
    (2799, 3052, 2861, 3054, 2876, 3888, 3006, 4018, 3249,),
    (2848, 2861, 2863, 3054, 2096, 3121, 3123, 3314,),
    (2913, 2926, 2991, 3043, 2161, 3184, 3186, 2291, 3124,),
    (2978, 2991, 2226, 3249, 3251, 3312, 3189, 3444,),
    (3071, 4083, 3312, 3121, 3314, 3124, 3381, 3254,),
    (3087, 971, 3123, 756, 3319, 3574, 3506, 3509, 3441,),
    (3186, 3189, 3444, 3339, 711, 3446, 3383, 3571, 504,),
    (3251, 3254, 3509, 3418, 1686, 3319, 3572, 3384, 1465,),
    (3327, 4091, 3831, 3572, 3574, 3832, 3641, 3701, 3514,),
    (3381, 3383, 3384, 3449, 3643, 3834, 3766,),
    (3446, 3465, 581, 3511, 3449, 3704, 3636, 3376, 378, 3579, 3132,),
    (3511, 3528, 516, 3514, 3769, 3704, 315, 3644, 3709,),
    (3579, 3832, 3834, 3769, 3644, 3901, 3774,),
    (3641, 3706, 3643, 3709, 3964, 3774, 3839,),
    (3670, 1426, 3706, 3771, 1213, 3964, 3966, 3903,),
    (3733, 1361, 3771, 3796, 1296, 1150, 4029, 1087, 4092,),
    (3839, 4092, 4094, 4029,),
    (3901, 3903, 4094,),
    (3966, 4031,),
    (4031,),
)


def programs():
    arrive = [{} for _ in range(BLOCKS)]
    send = [{} for _ in range(BLOCKS)]
    extra = [SPAN] * BLOCKS
    count = [0] * BLOCKS
    for block, hops in enumerate(TREES):
        slot, depth = {block: 0}, {block: 0}
        for hop in hops:
            src, dst = hop // BLOCKS, hop % BLOCKS
            depth[dst] = depth[src] + 1
            if 0 < dst - block < SPAN:
                slot[dst] = dst - block
            else:
                slot[dst] = extra[dst]
                extra[dst] += 1
            arrive[dst].setdefault(depth[dst], []).append(slot[dst])
            send[src].setdefault(slot[src], []).append((dst, slot[dst], depth[dst]))
            count[src] += 1
    deepest = max(max(a) for a in arrive if a)
    return arrive, send, max(extra), count, deepest


ARRIVE, SEND, SLOTS, SENDS, DEPTH = programs()
PARTS = 4
OFFSET = tuple(2 * d for d in range(DEPTH + 1))


def kernel(heads, group, blk_count,
           docs, q_hbm, k_hbm, v_hbm, o_hbm,
           window, q_all, o_all, bias,
           own_sem, q_sem, o_sem, send_sem, recv_sem):
    blk, half = lax.axis_index("blk"), lax.axis_index("head")
    me = jnp.where(half == 0, blk, BLOCKS - 1 - blk)
    z_hi, x, y = blk // 16, lax.rem(blk // 4, 4), lax.rem(blk, 4)

    def own_copy(u, h):
        cols = pl.ds(pl.multiple_of(h * D, D), D)
        return pltpu.make_async_copy(
            (k_hbm, v_hbm)[u].at[:, cols], window.at[h, 0, u], own_sem.at[u, h])

    def q_copy(h):
        cols = pl.ds(pl.multiple_of(h * group * D, group * D), group * D)
        return pltpu.make_async_copy(q_hbm.at[:, cols], q_all.at[h], q_sem.at[h])

    def o_copy(h):
        cols = pl.ds(pl.multiple_of(h * group * D, group * D), group * D)
        return pltpu.make_async_copy(o_all.at[h], o_hbm.at[:, cols], o_sem.at[h])

    def hop(h, s_slot, d_slot, there, depth):
        early = there < BLOCKS // 2
        return pltpu.make_async_remote_copy(
            src_ref=window.at[h, s_slot], dst_ref=window.at[h, d_slot],
            send_sem=send_sem.at[0], recv_sem=recv_sem.at[h, depth - 1],
            device_id={"blk": there if early else BLOCKS - 1 - there, "head": 0 if early else 1},
            device_id_type=MESH)

    def wait_bytes(ref, sem):
        pltpu.make_async_copy(ref, ref, sem).wait()

    def on_block(body, low=0, high=BLOCKS):
        if high - low == 1:
            return body(low)
        mid = (low + high) // 2

        @pl.when(me < mid)
        def _():
            on_block(body, low, mid)

        @pl.when(me >= mid)
        def _():
            on_block(body, mid, high)

    barrier = pltpu.get_barrier_semaphore()
    for dx, dy, dz in [tuple(hops * (axis == at) for at in range(3))
                       for axis in range(3) for hops in (1, 2, 3)]:
        z = lax.rem(2 * z_hi + half + dz, 4)
        there = {"blk": z // 2 * 16 + lax.rem(x + dx, 4) * 4 + lax.rem(y + dy, 4),
                 "head": lax.rem(z, 2)}
        pl.semaphore_signal(barrier, inc=1, device_id=there, device_id_type=MESH)

    @pl.loop(0, heads)
    def _(h):
        for u in range(2):
            own_copy(u, h).start()

    my_doc = docs[me]
    for slot in range(SPAN):
        at = me - slot
        same = (at >= 0) & (docs[jnp.maximum(at, 0)] == my_doc)
        bias[slot * T:(slot + 1) * T] = jnp.where(
            lax.broadcasted_iota(jnp.int32, (T, D), 1) == 0,
            jnp.where(same, 0.0, -1e30), 0.0).astype(jnp.bfloat16)

        @pl.when(at < 0)
        def _(slot=slot):
            @pl.loop(0, heads)
            def _(h):
                window[h, slot] = jnp.zeros((2, T, D), jnp.bfloat16)

    pl.semaphore_wait(barrier, 9)

    lane = lax.broadcasted_iota(jnp.int32, (1, D), 1)
    factor = math.log2(math.e) / math.sqrt(D)

    def attend(h, part, parts):
        count = group // parts
        first = part * count
        key = jnp.concatenate([window[h, :SPAN, 0].reshape(SPAN * T, D), bias[...]], axis=1)
        value = jnp.concatenate(
            [window[h, :SPAN, 1].reshape(SPAN * T, D),
             jnp.ones((SPAN * T, D), jnp.bfloat16)], axis=1)
        marker = jnp.broadcast_to(jnp.where(lane == 0, 1.0, 0.0), (count * T, D))
        query = jnp.concatenate(
            [jnp.concatenate([q_all[h, :, (first + g) * D:(first + g + 1) * D]
                              for g in range(count)], axis=0), marker.astype(jnp.bfloat16)], axis=1)
        row = lax.broadcasted_iota(jnp.int32, (1, T, T), 1)
        column = lax.broadcasted_iota(jnp.int32, (1, T, T), 2)
        causal = jnp.broadcast_to(column <= row, (count, T, T)).reshape(count * T, T)
        score = lax.dot_general(query, key, (((1,), (1,)), ((), ())),
                                preferred_element_type=jnp.float32)
        pieces = [jnp.where(causal, score[:, :T], -1e30)]
        pieces += [score[:, n * T:(n + 1) * T] for n in range(1, SPAN)]
        top = jnp.max(functools.reduce(jnp.maximum, pieces), axis=1, keepdims=True)
        weight = jnp.concatenate(
            [jnp.exp2((piece - top) * factor).astype(jnp.bfloat16) for piece in pieces], axis=1)
        summed = jnp.dot(weight, value, preferred_element_type=jnp.float32)
        out = (summed[:, :D] / summed[:, D:]).astype(jnp.bfloat16)
        for g in range(count):
            o_all[h, :, (first + g) * D:(first + g + 1) * D] = out[g * T:(g + 1) * T]

    ready = jnp.int32(0)
    for block in range(BLOCKS):
        ready = jnp.where(me == block, OFFSET[max(ARRIVE[block], default=0)], ready)

    @pl.loop(0, heads + OFFSET[DEPTH])
    def _(i):
        @pl.when(i < heads)
        def _():
            q_copy(i).start()
            for u in range(2):
                own_copy(u, i).wait()

        def travel(block):
            for depth in range(DEPTH, -1, -1):
                h = i - OFFSET[depth]
                slots = ARRIVE[block].get(depth, []) if depth else [0]
                if not slots:
                    continue

                @pl.when((h >= 0) & (h < heads))
                def _(h=h, slots=slots, depth=depth):
                    if depth:
                        wait_bytes(window.at[h, pl.ds(0, len(slots))], recv_sem.at[h, depth - 1])
                    for slot in slots:
                        for there, d_slot, later in SEND[block].get(slot, ()):
                            hop(h, slot, d_slot, there, later).start()

        on_block(travel)
        done = i - ready

        @pl.when((done >= 0) & (done < heads))
        def _():
            q_copy(done).wait()
            for part in range(PARTS):
                attend(done, part, PARTS)

            o_copy(done).start()

    def finish(block):
        if SENDS[block]:
            wait_bytes(window.at[:, pl.ds(0, SENDS[block])], send_sem.at[0])

    on_block(finish)

    @pl.loop(0, heads)
    def _(h):
        o_copy(h).wait()


def on_device(queries, keys, values, block_docs):
    blk_count = lax.axis_size("blk")
    heads = keys.shape[1] // D
    group = queries.shape[1] // keys.shape[1]
    anywhere = pl.BlockSpec(memory_space=pltpu.HBM)
    return pl.pallas_call(
        functools.partial(kernel, heads, group, blk_count),
        out_shape=jax.ShapeDtypeStruct(queries.shape, jnp.bfloat16),
        in_specs=[pl.BlockSpec(memory_space=pltpu.SMEM), anywhere, anywhere, anywhere],
        out_specs=anywhere,
        scratch_shapes=[
            pltpu.VMEM((heads, SLOTS, 2, T, D), jnp.bfloat16),
            pltpu.VMEM((heads, T, group * D), jnp.bfloat16),
            pltpu.VMEM((heads, T, group * D), jnp.bfloat16),
            pltpu.VMEM((SPAN * T, D), jnp.bfloat16),
            pltpu.SemaphoreType.DMA((2, heads)),
            pltpu.SemaphoreType.DMA((heads,)),
            pltpu.SemaphoreType.DMA((heads,)),
            pltpu.SemaphoreType.DMA((1,)),
            pltpu.SemaphoreType.DMA((heads, DEPTH)),
        ],
        compiler_params=pltpu.CompilerParams(
            collective_id=0, has_side_effects=True, vmem_limit_bytes=62 << 20),
        name="window_attention",
    )(block_docs, queries, keys, values)


def solution(mesh):
    rows = P(("dp", "blk", "head"), None)
    return jax.shard_map(
        on_device, mesh=mesh, in_specs=(rows, rows, rows, P("dp")), out_specs=rows,
        check_vma=False)
```
